32 devices in a mesh: grp: 2 (over y), pts: 8 (over z, x), rcv: 2 (over core).
Axes of the slice: x: 2, y: 2, z: 4, core: 2. Of those that a mesh axis runs over, the one named last changes fastest.
Arguments:
- src_green: float32 [2, 128, 2048], P(None, 'grp', 'pts'), parts along dimension 1, may hold values from -0.125 to 0.125
- rcv_green: float32 [2, 2048, 2048], P(None, ('grp', 'rcv'), 'pts'), parts along dimension 1, may hold values from -6 to 6
- model: float32 [4096], P(('grp', 'pts')), parts along dimension 0, may hold values from -6 to 6
- observed: float32 [128, 2, 1024], P(('grp', 'pts'), None, 'rcv'), parts along dimension 0, may hold values from -30 to 30, as said below
Outputs:
- gradient: float32 [4096], P(('grp', 'pts')), parts along dimension 0
The draws below stay inside these ranges and needn't reach their ends.
There are 2 independent parts, one for each index of `grp`. The reference program is written for one: setup_inputs(seed, part) draws one part's arguments, and reference() takes and returns one part's arrays. A program takes and returns all parts, laid end to end along the dimension named above; each array names one. Nothing has to cross between parts.
Inputs may be any that keep to these rules, and one draw needn't show every extreme that they name: `observed`: complex data (real and imaginary parts) whose scale varies with the source.
All inputs are finite; a program needn't handle non-finite values.
Results may differ from the reference program's by a relative error of at most 0.000068.
Values sent between devices are 32-bit elements; how exact they have to be, the bound alone decides.
A program may use at most 64 MiB of HBM per device.

```python
import jax
import jax.numpy as jnp
from jax import lax

POINTS = 2048
RECEIVERS = 1024
SOURCES = 64


def draw_observed(key, part):
    key_base, key_jitter = jax.random.split(jax.random.fold_in(key, 7), 2)
    ramp = 3.0 ** (jnp.arange(SOURCES, dtype=jnp.float32) / SOURCES)
    ramp = ramp.reshape(SOURCES, 1, 1)
    jitter = jax.random.uniform(key_jitter, (SOURCES, 1, 1), jnp.float32, 0.7, 1.4)
    base = jnp.clip(jax.random.normal(key_base, (SOURCES, 2, RECEIVERS), jnp.float32), -6.0, 6.0) * 0.5
    return (base * ramp * jitter).astype(jnp.float32)


def shard_levels(own_key, shape, cuts, low, top_value):
    gain = 1.0
    for position, shards_of in cuts:
        draws = jax.random.uniform(jax.random.fold_in(jax.random.fold_in(own_key, 6), position), (shards_of,), jnp.float32, low / len(cuts), top_value / len(cuts))
        gain = gain * jnp.repeat(jnp.exp(draws), shape[position] // shards_of).reshape((-1,) + (1,) * (len(shape) - 1 - position))
    return gain


def scatter_about(rng, extent, width, most, pieces=(), kind=jnp.bfloat16):
    factor_of = shard_levels(rng, extent, pieces, -0.22, 0.18) if pieces else 1.0
    drawn = jax.random.normal(rng, extent, jnp.float32) * width * factor_of
    return jnp.minimum(jnp.maximum(drawn, -most), most).astype(kind)


def setup_inputs(seed: int = 0, part: int = 0) -> dict:
    key_of = jax.random.split(jax.random.key(seed), 5)
    part_splits = jax.random.split(jax.random.fold_in(key_of[4], part), 5)
    src_green = scatter_about(part_splits[0], (2, SOURCES, POINTS), POINTS ** -0.5, 0.125, ((2, 8),), jnp.float32)
    rcv_green = scatter_about(part_splits[1], (2, RECEIVERS, POINTS), 1.0, 6.0, ((1, 2), (2, 8)), jnp.float32)
    model = scatter_about(part_splits[2], (POINTS,), 1.0, 6.0, ((0, 8),), jnp.float32)
    observed = draw_observed(jax.random.fold_in(jax.random.fold_in(key_of[4], part), 71), part)
    return dict(src_green=src_green, rcv_green=rcv_green, model=model, observed=observed)


def modelled_data(scaled, rcv_green):
    highest = lax.Precision.HIGHEST
    real_part = jnp.dot(scaled[0], rcv_green[0].T, precision=highest, preferred_element_type=jnp.float32) - jnp.dot(scaled[1], rcv_green[1].T, precision=highest, preferred_element_type=jnp.float32)
    imag_part = jnp.dot(scaled[0], rcv_green[1].T, precision=highest, preferred_element_type=jnp.float32) + jnp.dot(scaled[1], rcv_green[0].T, precision=highest, preferred_element_type=jnp.float32)
    return jnp.stack([real_part, imag_part], axis=1)

def image_terms(weighted, rcv_green, src_rows):
    highest = lax.Precision.HIGHEST
    back_real = jnp.dot(weighted[:, 0, :], rcv_green[0], precision=highest, preferred_element_type=jnp.float32) + jnp.dot(weighted[:, 1, :], rcv_green[1], precision=highest, preferred_element_type=jnp.float32)
    back_imag = jnp.dot(weighted[:, 1, :], rcv_green[0], precision=highest, preferred_element_type=jnp.float32) - jnp.dot(weighted[:, 0, :], rcv_green[1], precision=highest, preferred_element_type=jnp.float32)
    return lax.optimization_barrier(jnp.sum(src_rows[0] * back_real + src_rows[1] * back_imag, axis=0))

def reference(src_green, rcv_green, model, observed):
    scaled = src_green * model[None, None, :]
    modelled = modelled_data(scaled, rcv_green)
    resid = modelled - observed
    energy = resid[:, 0, :] ** 2 + resid[:, 1, :] ** 2
    spread_sq = jnp.sum(energy) / (SOURCES * RECEIVERS) + 1e-06
    weighted = resid / (1.0 + energy / spread_sq)[:, None, :]
    gradient = image_terms(weighted, rcv_green, src_green)
    return gradient * jnp.sqrt(jnp.float32(POINTS) / (RECEIVERS * SOURCES))
```

```python
import functools
import math

import jax
import jax.numpy as jnp
from jax import lax
from jax.experimental import pallas as pl
from jax.experimental.pallas import tpu as pltpu
from jax.sharding import PartitionSpec as P

MESH = pl.DeviceIdType.MESH
UNROLL = 32
CHUNK = 64


def repeat(start, stop, body):
    if stop - start <= UNROLL:
        for i in range(start, stop):
            body(i)
    else:

        @pl.loop(start, stop)
        def _(i):
            body(i)


def split(a):
    high = a.astype(jnp.bfloat16)
    low = (a - high.astype(jnp.float32)).astype(jnp.bfloat16)
    return high, low


def product(a, b_high, b_low, b_axis):
    rows = a.shape[0]
    a_high, a_low = split(a)
    dims = (((1,), (b_axis,)), ((), ()))
    both = lax.dot_general(
        jnp.concatenate([a_high, a_low], axis=0), b_high, dims, preferred_element_type=jnp.float32
    )
    cross = lax.dot_general(a_high, b_low, dims, preferred_element_type=jnp.float32)
    return both[:rows] + (both[rows:] + cross)


def near_first(z, nz):
    if nz > 8:
        return [jnp.int32(j) for j in range(1, nz)]
    table = []
    for here in range(nz):
        others = sorted((abs(o - here), o) for o in range(nz) if o != here)
        table.append([(o - here) % nz for _, o in others])
    order = []
    for k in range(nz - 1):
        j = jnp.int32(table[0][k])
        for here in range(1, nz):
            j = jnp.where(z == here, jnp.int32(table[here][k]), j)
        order.append(j)
    return order


def kernel(
    nx, nz, nr, scale,
    src_hbm, rcv_hbm, model_hbm, obs_hbm, out_ref,
    src, rcv, model, obs, b_high, b_low, part, xbuf, zsend, zbuf, gath, own_energy, ebuf, img, img_in,
    load, xs, xr, zs, zr, gs, gr, hs, hr, es, er, ims, imr,
):
    n = nx * nz
    total = n * nr
    p = lax.axis_index("pts")
    c = lax.axis_index("rcv")
    z, x = p // nx, p % nx
    q = p * nr + c
    sources = src.shape[1]
    receivers = rcv.shape[1]
    block = part.shape[2]

    loads = [
        pltpu.make_async_copy(src_hbm, src, load.at[0]),
        pltpu.make_async_copy(model_hbm, model, load.at[1]),
        pltpu.make_async_copy(rcv_hbm.at[0], rcv.at[0], load.at[2]),
        pltpu.make_async_copy(rcv_hbm.at[1], rcv.at[1], load.at[3]),
        pltpu.make_async_copy(obs_hbm, obs, load.at[4]),
    ]
    for copy in loads:
        copy.start()

    barrier = pltpu.get_barrier_semaphore()

    def greet(o):
        to = (q + o) % total
        pl.semaphore_signal(
            barrier, inc=1, device_id={"pts": to // nr, "rcv": to % nr}, device_id_type=MESH
        )

    repeat(1, total, greet)

    for copy in loads[:3]:
        copy.wait()
    b_high[0], b_low[0] = split(rcv[0])
    loads[3].wait()
    b_high[1], b_low[1] = split(rcv[1])

    chunk = CHUNK if sources % CHUNK == 0 else sources

    def model_chunk(i):
        rows = pl.ds(i * chunk, chunk)
        weight = model[...]
        scaled = jnp.concatenate([src[0, rows] * weight, src[1, rows] * weight], axis=0)
        with_real = product(scaled, b_high[0], b_low[0], 1)
        with_imag = product(scaled, b_high[1], b_low[1], 1)
        real = with_real[:chunk] - with_imag[chunk:]
        imag = with_imag[:chunk] + with_real[chunk:]
        blocks = pl.ds(i * (chunk // block), chunk // block)
        part[blocks, 0] = real.reshape(chunk // block, block, receivers)
        part[blocks, 1] = imag.reshape(chunk // block, block, receivers)

    if sources == chunk:
        model_chunk(0)
    else:
        pl.loop(0, sources // chunk)(model_chunk)

    pl.semaphore_wait(barrier, total - 1)

    order = near_first(z, nz)
    far = order[::-1]

    def to_x(source, target, send, recv, d):
        return pltpu.make_async_remote_copy(
            source, target, send, recv,
            device_id={"pts": z * nx + (x + d) % nx}, device_id_type=MESH,
        )

    def to_z(source, target, send, recv, j):
        return pltpu.make_async_remote_copy(
            source, target, send, recv,
            device_id={"pts": ((z + j) % nz) * nx + x}, device_id_type=MESH,
        )

    pending = []
    x_copies = []
    for j in far + [jnp.int32(0)]:
        row = []
        for d in range(1, nx):
            goal = ((z + j) % nz) * nx + (x + d) % nx
            copy = to_x(part.at[goal], xbuf.at[d - 1, j], xs.at[d - 1, j], xr.at[d - 1, j], d)
            copy.start()
            row.append(copy)
        x_copies.append(row)
    loads[4].wait()
    observed = [obs[:, part_of, :] for part_of in range(2)]
    z_copies = []
    for j, row in zip(far, x_copies):
        acc = part[((z + j) % nz) * nx + x]
        for d, copy in enumerate(row):
            copy.wait_recv()
            acc = acc + xbuf[d, j]
        zsend[j] = acc
        copy = to_z(zsend.at[j], zbuf.at[j], zs.at[j], zr.at[j], j)
        copy.start()
        z_copies.append(copy)
    acc = part[p]
    for d, copy in enumerate(x_copies[-1]):
        copy.wait_recv()
        acc = acc + xbuf[d, 0]
    back = [(nz - j) % nz for j in order]
    for j in back:
        to_z(zsend.at[j], zbuf.at[j], zs.at[j], zr.at[j], j).wait_recv()
        acc = acc + zbuf[j]
    for row in x_copies:
        pending += row
    pending += z_copies

    real = acc[0] - observed[0]
    imag = acc[1] - observed[1]
    gath[p, 0] = real
    gath[p, 1] = imag
    lanes = own_energy.shape[-1]
    energy = jnp.sum(real * real + imag * imag, axis=0, keepdims=True)
    narrow = energy[:, :lanes]
    for i in range(1, receivers // lanes):
        narrow = narrow + energy[:, i * lanes:(i + 1) * lanes]
    own_energy[0] = narrow

    for j in far:
        copy = to_z(gath.at[p], gath.at[p], gs.at[j], gr.at[j], j)
        copy.start()
        pending.append(copy)
    for d in range(1, nx):
        copy = to_x(gath.at[p], gath.at[p], hs.at[d - 1, 0], hr.at[d - 1, 0], d)
        copy.start()
        pending.append(copy)

    def tell(o):
        to = (q + o) % total
        pltpu.make_async_remote_copy(
            own_energy.at[0], ebuf.at[o - 1], es, er,
            device_id={"pts": to // nr, "rcv": to % nr}, device_id_type=MESH,
        ).start()

    repeat(1, total, tell)

    for j in back:
        origin = ((z - j + nz) % nz) * nx + x
        to_z(gath.at[origin], gath.at[origin], gs.at[j], gr.at[j], j).wait_recv()
        for d in range(1, nx):
            copy = to_x(gath.at[origin], gath.at[origin], hs.at[d - 1, j], hr.at[d - 1, j], d)
            copy.start()
            pending.append(copy)
    told = ebuf.at[pl.ds(0, total - 1)]
    pltpu.make_async_copy(told, told, er).wait()
    summed = jnp.sum(jnp.sum(ebuf[pl.ds(0, total - 1)], axis=0) + own_energy[0], axis=1, keepdims=True)
    spread_sq = summed / (sources * receivers * nr) + 1e-06
    inverse = 1.0 / spread_sq
    for j in [jnp.int32(0)] + back:
        for d in range(1, nx):
            origin = ((z - j + nz) % nz) * nx + (x - d + nx) % nx
            to_x(gath.at[origin], gath.at[origin], hs.at[d - 1, j], hr.at[d - 1, j], d).wait_recv()

    def image_chunk(i):
        rows = pl.ds(i * chunk, chunk)
        blocks = pl.ds(i * (chunk // block), chunk // block)
        real = gath[blocks, 0].reshape(chunk, receivers)
        imag = gath[blocks, 1].reshape(chunk, receivers)
        gain = 1.0 / (1.0 + (real * real + imag * imag) * inverse)
        weighted = jnp.concatenate([real * gain, imag * gain], axis=0)
        with_real = product(weighted, b_high[0], b_low[0], 0)
        with_imag = product(weighted, b_high[1], b_low[1], 0)
        back_real = with_real[:chunk] + with_imag[chunk:]
        back_imag = with_real[chunk:] - with_imag[:chunk]
        return jnp.sum(src[0, rows] * back_real + src[1, rows] * back_imag, axis=0, keepdims=True)

    if sources == chunk:
        image = image_chunk(0)
    else:
        image = lax.fori_loop(
            0, sources // chunk, lambda i, t: t + image_chunk(i), jnp.zeros(img.shape[1:], jnp.float32)
        )
    image = image * scale
    img[0] = image
    for d in range(1, nr):
        copy = pltpu.make_async_remote_copy(
            img.at[0], img_in.at[d - 1], ims.at[d - 1], imr.at[d - 1],
            device_id={"rcv": (c + d) % nr}, device_id_type=MESH,
        )
        copy.start()
        pending.append(copy)
    for copy in pending[len(pending) - (nr - 1):]:
        copy.wait_recv()
    for d in range(1, nr):
        image = image + img_in[d - 1]
    out_ref[...] = image
    for copy in pending:
        copy.wait_send()
    pltpu.make_async_copy(told, told, es).wait()


def local(src_green, rcv_green, model, observed):
    n = lax.axis_size("pts")
    nr = lax.axis_size("rcv")
    bits = n.bit_length() - 1
    nx = 2 ** ((bits + 1) // 4)
    if n % nx:
        nx = 1
    nz = n // nx
    sources, points = src_green.shape[1:]
    receivers = rcv_green.shape[1]
    block = observed.shape[0]
    scale = math.sqrt(points * n / (receivers * nr * sources))
    f32, bf16 = jnp.float32, jnp.bfloat16
    dma = pltpu.SemaphoreType.DMA
    lanes = 128 if receivers % 128 == 0 else receivers
    image = pl.pallas_call(
        functools.partial(kernel, nx, nz, nr, scale),
        out_shape=jax.ShapeDtypeStruct((1, points), f32),
        in_specs=[pl.BlockSpec(memory_space=pl.ANY)] * 4,
        out_specs=pl.BlockSpec(memory_space=pltpu.VMEM),
        scratch_shapes=[
            pltpu.VMEM(src_green.shape, f32),
            pltpu.VMEM(rcv_green.shape, f32),
            pltpu.VMEM((1, points), f32),
            pltpu.VMEM(observed.shape, f32),
            pltpu.VMEM(rcv_green.shape, bf16),
            pltpu.VMEM(rcv_green.shape, bf16),
            pltpu.VMEM((n, 2, block, receivers), f32),
            pltpu.VMEM((max(nx - 1, 1), nz, 2, block, receivers), f32),
            pltpu.VMEM((nz, 2, block, receivers), f32),
            pltpu.VMEM((nz, 2, block, receivers), f32),
            pltpu.VMEM((n, 2, block, receivers), f32),
            pltpu.VMEM((1, 1, lanes), f32),
            pltpu.VMEM((n * nr, 1, lanes), f32),
            pltpu.VMEM((1, 1, points), f32),
            pltpu.VMEM((max(nr - 1, 1), 1, points), f32),
            dma((5,)),
            dma((max(nx - 1, 1), nz)),
            dma((max(nx - 1, 1), nz)),
            dma((nz,)),
            dma((nz,)),
            dma((nz,)),
            dma((nz,)),
            dma((max(nx - 1, 1), nz)),
            dma((max(nx - 1, 1), nz)),
            dma(()),
            dma(()),
            dma((max(nr - 1, 1),)),
            dma((max(nr - 1, 1),)),
        ],
        compiler_params=pltpu.CompilerParams(collective_id=0, has_side_effects=True),
    )(src_green, rcv_green, model.reshape(1, points), observed)
    return image.reshape(points)


def solution(mesh):
    placed = (
        P(None, "grp", "pts"),
        P(None, ("grp", "rcv"), "pts"),
        P(("grp", "pts")),
        P(("grp", "pts"), None, "rcv"),
    )
    return jax.shard_map(
        local, mesh=mesh, in_specs=placed, out_specs=P(("grp", "pts")), check_vma=False
    )
```

```python
import functools
import math

import jax
import jax.numpy as jnp
from jax import lax
from jax.experimental import pallas as pl
from jax.experimental.pallas import tpu as pltpu
from jax.sharding import PartitionSpec as P

MESH = pl.DeviceIdType.MESH
UNROLL = 32


def repeat(start, stop, body):
    if stop - start <= UNROLL:
        for i in range(start, stop):
            body(i)
    else:

        @pl.loop(start, stop)
        def _(i):
            body(i)


def split(a):
    high = a.astype(jnp.bfloat16)
    low = (a - high.astype(jnp.float32)).astype(jnp.bfloat16)
    return high, low


def product(a, b_high, b_low, b_axis):
    rows = a.shape[0]
    a_high, a_low = split(a)
    dims = (((1,), (b_axis,)), ((), ()))
    both = lax.dot_general(
        jnp.concatenate([a_high, a_low], axis=0), b_high, dims, preferred_element_type=jnp.float32
    )
    cross = lax.dot_general(a_high, b_low, dims, preferred_element_type=jnp.float32)
    return both[:rows] + (both[rows:] + cross)


def near_first(z, nz):
    if nz > 8:
        return [jnp.int32(j) for j in range(1, nz)]
    table = []
    for here in range(nz):
        others = sorted((abs(o - here), o) for o in range(nz) if o != here)
        table.append([(o - here) % nz for _, o in others])
    order = []
    for k in range(nz - 1):
        j = jnp.int32(table[0][k])
        for here in range(1, nz):
            j = jnp.where(z == here, jnp.int32(table[here][k]), j)
        order.append(j)
    return order


def kernel(
    nx, nz, nr, scale,
    src_hbm, rcv_hbm, model_hbm, obs_hbm, out_ref,
    src, rcv, model, obs, b_high, b_low, part, xbuf, zsend, zbuf, gath, own_energy, ebuf, img, img_in,
    load, xs, xr, zs, zr, gs, gr, hs, hr, es, er, ims, imr, tokens,
):
    n = nx * nz
    total = n * nr
    p = lax.axis_index("pts")
    c = lax.axis_index("rcv")
    z, x = p // nx, p % nx
    q = p * nr + c
    sources = src.shape[1]
    receivers = rcv.shape[1]
    block = part.shape[3]

    loads = [
        pltpu.make_async_copy(src_hbm, src, load.at[0]),
        pltpu.make_async_copy(model_hbm, model, load.at[1]),
        pltpu.make_async_copy(rcv_hbm.at[0], rcv.at[0], load.at[2]),
        pltpu.make_async_copy(rcv_hbm.at[1], rcv.at[1], load.at[3]),
        pltpu.make_async_copy(obs_hbm, obs, load.at[4]),
    ]
    for copy in loads:
        copy.start()

    barrier = pltpu.get_barrier_semaphore()
    row_peers = nx * nr - 1
    below, above = (z + nz - 1) % nz, (z + 1) % nz

    def greet(device):
        pl.semaphore_signal(barrier, inc=1, device_id=device, device_id_type=MESH)

    for o in range(1, nx * nr):
        to = (x * nr + c + o) % (nx * nr)
        greet({"pts": z * nx + to // nr, "rcv": to % nr})

    @pl.when(z > 0)
    def _():
        greet({"pts": below * nx + x})

    @pl.when(z < nz - 1)
    def _():
        greet({"pts": above * nx + x})

    def pass_up():
        @pl.when(z > 0)
        def _():
            pl.semaphore_wait(tokens.at[0], 1)

        @pl.when(z < nz - 1)
        def _():
            pl.semaphore_signal(tokens.at[0], inc=1, device_id={"pts": above * nx + x}, device_id_type=MESH)

    def pass_down():
        @pl.when(z < nz - 1)
        def _():
            pl.semaphore_wait(tokens.at[1], 1)

        @pl.when(z > 0)
        def _():
            pl.semaphore_signal(tokens.at[1], inc=1, device_id={"pts": below * nx + x}, device_id_type=MESH)

    for copy in loads[:3]:
        copy.wait()
    b_high[0], b_low[0] = split(rcv[0])
    loads[3].wait()
    b_high[1], b_low[1] = split(rcv[1])

    rows = nz * block

    def sources_of(part_of, d):
        column = (x + d) % nx
        return jnp.concatenate(
            [src[part_of, pl.ds(pl.multiple_of((k * nx + column) * block, block), block)] for k in range(nz)],
            axis=0,
        )

    def model_column(d):
        weight = model[...]
        scaled = jnp.concatenate([sources_of(0, d) * weight, sources_of(1, d) * weight], axis=0)
        with_real = product(scaled, b_high[0], b_low[0], 1)
        with_imag = product(scaled, b_high[1], b_low[1], 1)
        part[d, :, 0] = (with_real[:rows] - with_imag[rows:]).reshape(nz, block, receivers)
        part[d, :, 1] = (with_imag[:rows] + with_real[rows:]).reshape(nz, block, receivers)

    order = near_first(z, nz)
    far = order[::-1]

    def to_x(source, target, send, recv, d):
        return pltpu.make_async_remote_copy(
            source, target, send, recv,
            device_id={"pts": z * nx + (x + d) % nx}, device_id_type=MESH,
        )

    def to_z(source, target, send, recv, j):
        return pltpu.make_async_remote_copy(
            source, target, send, recv,
            device_id={"pts": ((z + j) % nz) * nx + x}, device_id_type=MESH,
        )

    pending = []
    x_copies = [[] for _ in range(nz)]
    for d in range(1, nx):
        model_column(d)
        if d == 1:
            pl.semaphore_wait(barrier, row_peers + jnp.minimum(z, 1) + jnp.minimum(nz - 1 - z, 1))
        for k, j in enumerate(far + [jnp.int32(0)]):
            copy = to_x(part.at[d, (z + j) % nz], xbuf.at[d - 1, j], xs.at[d - 1, j], xr.at[d - 1, j], d)
            copy.start()
            x_copies[k].append(copy)
    model_column(0)
    if nx == 1:
        pl.semaphore_wait(barrier, row_peers + jnp.minimum(z, 1) + jnp.minimum(nz - 1 - z, 1))

    @pl.when(z < nz // 2)
    def _():
        pass_up()
        pass_down()

    @pl.when(z >= nz // 2)
    def _():
        pass_down()
        pass_up()

    loads[4].wait()
    observed = [obs[:, part_of, :] for part_of in range(2)]
    z_copies = []
    for j, row in zip(far, x_copies):
        acc = part[0, (z + j) % nz]
        for d, copy in enumerate(row):
            copy.wait_recv()
            acc = acc + xbuf[d, j]
        zsend[j] = acc
        copy = to_z(zsend.at[j], zbuf.at[j], zs.at[j], zr.at[j], j)
        copy.start()
        z_copies.append(copy)
    acc = part[0, z]
    for d, copy in enumerate(x_copies[-1]):
        copy.wait_recv()
        acc = acc + xbuf[d, 0]
    back = [(nz - j) % nz for j in order]
    for j in back:
        to_z(zsend.at[j], zbuf.at[j], zs.at[j], zr.at[j], j).wait_recv()
        acc = acc + zbuf[j]
    for row in x_copies:
        pending += row
    pending += z_copies

    real = acc[0] - observed[0]
    imag = acc[1] - observed[1]
    gath[0, z, 0] = real
    gath[0, z, 1] = imag
    lanes = own_energy.shape[-1]
    energy = jnp.sum(real * real + imag * imag, axis=0, keepdims=True)
    narrow = energy[:, :lanes]
    for i in range(1, receivers // lanes):
        narrow = narrow + energy[:, i * lanes:(i + 1) * lanes]
    own_energy[0] = narrow

    for j in far:
        copy = to_z(gath.at[0, z], gath.at[0, z], gs.at[j], gr.at[j], j)
        copy.start()
        pending.append(copy)
    for d in range(1, nx):
        copy = to_x(gath.at[0, z], gath.at[d, z], hs.at[d - 1, 0], hr.at[d - 1, 0], d)
        copy.start()
        pending.append(copy)

    def tell(o):
        to = (q + o) % total
        pltpu.make_async_remote_copy(
            own_energy.at[0], ebuf.at[o - 1], es, er,
            device_id={"pts": to // nr, "rcv": to % nr}, device_id_type=MESH,
        ).start()

    repeat(1, total, tell)

    for j in back:
        origin = (z - j + nz) % nz
        to_z(gath.at[0, origin], gath.at[0, origin], gs.at[j], gr.at[j], j).wait_recv()
        for d in range(1, nx):
            copy = to_x(gath.at[0, origin], gath.at[d, origin], hs.at[d - 1, j], hr.at[d - 1, j], d)
            copy.start()
            pending.append(copy)
    told = ebuf.at[pl.ds(0, total - 1)]
    pltpu.make_async_copy(told, told, er).wait()
    summed = jnp.sum(jnp.sum(ebuf[pl.ds(0, total - 1)], axis=0) + own_energy[0], axis=1, keepdims=True)
    spread_sq = summed / (sources * receivers * nr) + 1e-06
    inverse = 1.0 / spread_sq

    def image_column(d):
        real = gath[d, :, 0].reshape(rows, receivers)
        imag = gath[d, :, 1].reshape(rows, receivers)
        gain = 1.0 / (1.0 + (real * real + imag * imag) * inverse)
        weighted = jnp.concatenate([real * gain, imag * gain], axis=0)
        with_real = product(weighted, b_high[0], b_low[0], 0)
        with_imag = product(weighted, b_high[1], b_low[1], 0)
        back_real = with_real[:rows] + with_imag[rows:]
        back_imag = with_real[rows:] - with_imag[:rows]
        terms = sources_of(0, nx - d) * back_real + sources_of(1, nx - d) * back_imag
        return jnp.sum(terms, axis=0, keepdims=True)

    image = image_column(0)
    for d in range(1, nx):
        for j in [jnp.int32(0)] + back:
            origin = (z - j + nz) % nz
            to_x(gath.at[0, origin], gath.at[d, origin], hs.at[d - 1, j], hr.at[d - 1, j], d).wait_recv()
        image = image + image_column(d)
    image = image * scale
    img[0] = image
    for d in range(1, nr):
        copy = pltpu.make_async_remote_copy(
            img.at[0], img_in.at[d - 1], ims.at[d - 1], imr.at[d - 1],
            device_id={"rcv": (c + d) % nr}, device_id_type=MESH,
        )
        copy.start()
        pending.append(copy)
    for copy in pending[len(pending) - (nr - 1):]:
        copy.wait_recv()
    for d in range(1, nr):
        image = image + img_in[d - 1]
    out_ref[...] = image
    for copy in pending:
        copy.wait_send()
    pltpu.make_async_copy(told, told, es).wait()


def local(src_green, rcv_green, model, observed):
    n = lax.axis_size("pts")
    nr = lax.axis_size("rcv")
    bits = n.bit_length() - 1
    nx = 2 ** ((bits + 1) // 4)
    if n % nx:
        nx = 1
    nz = n // nx
    sources, points = src_green.shape[1:]
    receivers = rcv_green.shape[1]
    block = observed.shape[0]
    scale = math.sqrt(points * n / (receivers * nr * sources))
    f32, bf16 = jnp.float32, jnp.bfloat16
    dma = pltpu.SemaphoreType.DMA
    lanes = 128 if receivers % 128 == 0 else receivers
    image = pl.pallas_call(
        functools.partial(kernel, nx, nz, nr, scale),
        out_shape=jax.ShapeDtypeStruct((1, points), f32),
        in_specs=[pl.BlockSpec(memory_space=pl.ANY)] * 4,
        out_specs=pl.BlockSpec(memory_space=pltpu.VMEM),
        scratch_shapes=[
            pltpu.VMEM(src_green.shape, f32),
            pltpu.VMEM(rcv_green.shape, f32),
            pltpu.VMEM((1, points), f32),
            pltpu.VMEM(observed.shape, f32),
            pltpu.VMEM(rcv_green.shape, bf16),
            pltpu.VMEM(rcv_green.shape, bf16),
            pltpu.VMEM((nx, nz, 2, block, receivers), f32),
            pltpu.VMEM((max(nx - 1, 1), nz, 2, block, receivers), f32),
            pltpu.VMEM((nz, 2, block, receivers), f32),
            pltpu.VMEM((nz, 2, block, receivers), f32),
            pltpu.VMEM((nx, nz, 2, block, receivers), f32),
            pltpu.VMEM((1, 1, lanes), f32),
            pltpu.VMEM((n * nr, 1, lanes), f32),
            pltpu.VMEM((1, 1, points), f32),
            pltpu.VMEM((max(nr - 1, 1), 1, points), f32),
            dma((5,)),
            dma((max(nx - 1, 1), nz)),
            dma((max(nx - 1, 1), nz)),
            dma((nz,)),
            dma((nz,)),
            dma((nz,)),
            dma((nz,)),
            dma((max(nx - 1, 1), nz)),
            dma((max(nx - 1, 1), nz)),
            dma(()),
            dma(()),
            dma((max(nr - 1, 1),)),
            dma((max(nr - 1, 1),)),
            pltpu.SemaphoreType.REGULAR((2,)),
        ],
        compiler_params=pltpu.CompilerParams(collective_id=0, has_side_effects=True),
    )(src_green, rcv_green, model.reshape(1, points), observed)
    return image.reshape(points)


def solution(mesh):
    placed = (
        P(None, "grp", "pts"),
        P(None, ("grp", "rcv"), "pts"),
        P(("grp", "pts")),
        P(("grp", "pts"), None, "rcv"),
    )
    return jax.shard_map(
        local, mesh=mesh, in_specs=placed, out_specs=P(("grp", "pts")), check_vma=False
    )
```

```python
import functools
import math

import jax
import jax.numpy as jnp
from jax import lax
from jax.experimental import pallas as pl
from jax.experimental.pallas import tpu as pltpu
from jax.sharding import PartitionSpec as P

MESH = pl.DeviceIdType.MESH
UNROLL = 32


def repeat(start, stop, body):
    if stop - start <= UNROLL:
        for i in range(start, stop):
            body(i)
    else:

        @pl.loop(start, stop)
        def _(i):
            body(i)


def split(a):
    high = a.astype(jnp.bfloat16)
    low = (a - high.astype(jnp.float32)).astype(jnp.bfloat16)
    return high, low


def product(a, b_high, b_low, b_axis):
    rows = a.shape[0]
    a_high, a_low = split(a)
    dims = (((1,), (b_axis,)), ((), ()))
    both = lax.dot_general(
        jnp.concatenate([a_high, a_low], axis=0), b_high, dims, preferred_element_type=jnp.float32
    )
    cross = lax.dot_general(a_high, b_low, dims, preferred_element_type=jnp.float32)
    return both[:rows] + (both[rows:] + cross)


def near_first(z, nz):
    if nz > 8:
        return [jnp.int32(j) for j in range(1, nz)]
    table = []
    for here in range(nz):
        others = sorted((abs(o - here), o) for o in range(nz) if o != here)
        table.append([(o - here) % nz for _, o in others])
    order = []
    for k in range(nz - 1):
        j = jnp.int32(table[0][k])
        for here in range(1, nz):
            j = jnp.where(z == here, jnp.int32(table[here][k]), j)
        order.append(j)
    return order


def kernel(
    nx, nz, nr, scale,
    src_hbm, rcv_hbm, model_hbm, obs_hbm, out_ref,
    src, rcv, model, obs, b_high, b_low, part, xbuf, zsend, zbuf, gath, own_energy, ebuf, img, img_in,
    load, xs, xr, zs, zr, gs, gr, hs, hr, es, er, ims, imr, tokens,
):
    n = nx * nz
    total = n * nr
    p = lax.axis_index("pts")
    c = lax.axis_index("rcv")
    z, x = p // nx, p % nx
    q = p * nr + c
    sources = src.shape[1]
    receivers = rcv.shape[1]

    halves, _, block, width = part.shape[2:]
    cuts = [pl.ds(h * width, width) for h in range(halves)]
    loads = [
        pltpu.make_async_copy(src_hbm, src, load.at[0]),
        pltpu.make_async_copy(model_hbm, model, load.at[1]),
        pltpu.make_async_copy(obs_hbm, obs, load.at[2]),
    ]
    half_loads = [
        pltpu.make_async_copy(rcv_hbm.at[:, cut], rcv.at[:, cut], load.at[3 + h])
        for h, cut in enumerate(cuts)
    ]
    for copy in loads[:2] + half_loads + loads[2:]:
        copy.start()

    barrier = pltpu.get_barrier_semaphore()
    row_peers = nx * nr - 1
    below, above = (z + nz - 1) % nz, (z + 1) % nz

    def greet(device):
        pl.semaphore_signal(barrier, inc=1, device_id=device, device_id_type=MESH)

    for o in range(1, nx * nr):
        to = (x * nr + c + o) % (nx * nr)
        greet({"pts": z * nx + to // nr, "rcv": to % nr})

    @pl.when(z > 0)
    def _():
        greet({"pts": below * nx + x})

    @pl.when(z < nz - 1)
    def _():
        greet({"pts": above * nx + x})

    def pass_up():
        @pl.when(z > 0)
        def _():
            pl.semaphore_wait(tokens.at[0], 1)

        @pl.when(z < nz - 1)
        def _():
            pl.semaphore_signal(tokens.at[0], inc=1, device_id={"pts": above * nx + x}, device_id_type=MESH)

    def pass_down():
        @pl.when(z < nz - 1)
        def _():
            pl.semaphore_wait(tokens.at[1], 1)

        @pl.when(z > 0)
        def _():
            pl.semaphore_signal(tokens.at[1], inc=1, device_id={"pts": below * nx + x}, device_id_type=MESH)

    for copy in loads[:2]:
        copy.wait()
    rows = nz * block

    def sources_of(part_of, d):
        column = (x + d) % nx
        return jnp.concatenate(
            [src[part_of, pl.ds(pl.multiple_of((k * nx + column) * block, block), block)] for k in range(nz)],
            axis=0,
        )

    def model_column(d, h):
        weight = model[...]
        scaled = jnp.concatenate([sources_of(0, d) * weight, sources_of(1, d) * weight], axis=0)
        with_real = product(scaled, b_high[0, cuts[h]], b_low[0, cuts[h]], 1)
        with_imag = product(scaled, b_high[1, cuts[h]], b_low[1, cuts[h]], 1)
        part[d, :, h, 0] = (with_real[:rows] - with_imag[rows:]).reshape(nz, block, width)
        part[d, :, h, 1] = (with_imag[:rows] + with_real[rows:]).reshape(nz, block, width)

    order = near_first(z, nz)
    far = order[::-1]

    def to_x(source, target, send, recv, d):
        return pltpu.make_async_remote_copy(
            source, target, send, recv,
            device_id={"pts": z * nx + (x + d) % nx}, device_id_type=MESH,
        )

    def to_z(source, target, send, recv, j):
        return pltpu.make_async_remote_copy(
            source, target, send, recv,
            device_id={"pts": ((z + j) % nz) * nx + x}, device_id_type=MESH,
        )

    pending = []
    x_copies = [[[] for _ in range(nz)] for _ in range(halves)]
    for h in range(halves):
        half_loads[h].wait()
        for of in range(2):
            b_high[of, cuts[h]], b_low[of, cuts[h]] = split(rcv[of, cuts[h]])
        for d in range(1, nx):
            model_column(d, h)
            if h == 0 and d == 1:
                pl.semaphore_wait(barrier, row_peers + jnp.minimum(z, 1) + jnp.minimum(nz - 1 - z, 1))
            for k, j in enumerate(far + [jnp.int32(0)]):
                copy = to_x(
                    part.at[d, (z + j) % nz, h], xbuf.at[d - 1, j, h],
                    xs.at[d - 1, j, h], xr.at[d - 1, j, h], d,
                )
                copy.start()
                x_copies[h][k].append(copy)
    for h in range(halves):
        model_column(0, h)
    if nx == 1:
        pl.semaphore_wait(barrier, row_peers + jnp.minimum(z, 1) + jnp.minimum(nz - 1 - z, 1))

    @pl.when(z < nz // 2)
    def _():
        pass_up()
        pass_down()

    @pl.when(z >= nz // 2)
    def _():
        pass_down()
        pass_up()

    loads[2].wait()
    z_copies = []
    for h in range(halves):
        for j, row in zip(far, x_copies[h]):
            acc = part[0, (z + j) % nz, h]
            for d, copy in enumerate(row):
                copy.wait_recv()
                acc = acc + xbuf[d, j, h]
            zsend[j, h] = acc
            copy = to_z(zsend.at[j, h], zbuf.at[j, h], zs.at[j, h], zr.at[j, h], j)
            copy.start()
            z_copies.append(copy)
    back = [(nz - j) % nz for j in order]
    energy = None
    for h in range(halves):
        acc = part[0, z, h]
        for d, copy in enumerate(x_copies[h][-1]):
            copy.wait_recv()
            acc = acc + xbuf[d, 0, h]
        for j in back:
            to_z(zsend.at[j, h], zbuf.at[j, h], zs.at[j, h], zr.at[j, h], j).wait_recv()
            acc = acc + zbuf[j, h]
        real = acc[0] - obs[:, 0, cuts[h]]
        imag = acc[1] - obs[:, 1, cuts[h]]
        gath[0, z, h, 0] = real
        gath[0, z, h, 1] = imag
        own = gath.at[0, z, h]
        for j in far:
            copy = to_z(own, own, gs.at[j, h], gr.at[j, h], j)
            copy.start()
            pending.append(copy)
        for d in range(1, nx):
            copy = to_x(own, gath.at[d, z, h], hs.at[d - 1, 0, h], hr.at[d - 1, 0, h], d)
            copy.start()
            pending.append(copy)
        of_half = jnp.sum(real * real + imag * imag, axis=0, keepdims=True)
        energy = of_half if energy is None else energy + of_half
    for row in x_copies:
        for copies in row:
            pending += copies
    pending += z_copies
    lanes = own_energy.shape[-1]
    narrow = energy[:, :lanes]
    for i in range(1, width // lanes):
        narrow = narrow + energy[:, i * lanes:(i + 1) * lanes]
    own_energy[0] = narrow

    def tell(o):
        to = (q + o) % total
        pltpu.make_async_remote_copy(
            own_energy.at[0], ebuf.at[o - 1], es, er,
            device_id={"pts": to // nr, "rcv": to % nr}, device_id_type=MESH,
        ).start()

    repeat(1, total, tell)

    for h in range(halves):
        for j in back:
            origin = (z - j + nz) % nz
            landed = gath.at[0, origin, h]
            to_z(landed, landed, gs.at[j, h], gr.at[j, h], j).wait_recv()
            for d in range(1, nx):
                copy = to_x(landed, gath.at[d, origin, h], hs.at[d - 1, j, h], hr.at[d - 1, j, h], d)
                copy.start()
                pending.append(copy)
    told = ebuf.at[pl.ds(0, total - 1)]
    pltpu.make_async_copy(told, told, er).wait()
    summed = jnp.sum(jnp.sum(ebuf[pl.ds(0, total - 1)], axis=0) + own_energy[0], axis=1, keepdims=True)
    spread_sq = summed / (sources * receivers * nr) + 1e-06
    inverse = 1.0 / spread_sq

    def image_column(d, h):
        real = gath[d, :, h, 0].reshape(rows, width)
        imag = gath[d, :, h, 1].reshape(rows, width)
        gain = 1.0 / (1.0 + (real * real + imag * imag) * inverse)
        weighted = jnp.concatenate([real * gain, imag * gain], axis=0)
        with_real = product(weighted, b_high[0, cuts[h]], b_low[0, cuts[h]], 0)
        with_imag = product(weighted, b_high[1, cuts[h]], b_low[1, cuts[h]], 0)
        back_real = with_real[:rows] + with_imag[rows:]
        back_imag = with_real[rows:] - with_imag[:rows]
        terms = sources_of(0, nx - d) * back_real + sources_of(1, nx - d) * back_imag
        return jnp.sum(terms, axis=0, keepdims=True)

    image = image_column(0, 0)
    for h in range(1, halves):
        image = image + image_column(0, h)
    for h in range(halves):
        for d in range(1, nx):
            for j in [jnp.int32(0)] + back:
                origin = (z - j + nz) % nz
                to_x(
                    gath.at[0, origin, h], gath.at[d, origin, h],
                    hs.at[d - 1, j, h], hr.at[d - 1, j, h], d,
                ).wait_recv()
            image = image + image_column(d, h)
    image = image * scale
    img[0] = image
    for d in range(1, nr):
        copy = pltpu.make_async_remote_copy(
            img.at[0], img_in.at[d - 1], ims.at[d - 1], imr.at[d - 1],
            device_id={"rcv": (c + d) % nr}, device_id_type=MESH,
        )
        copy.start()
        pending.append(copy)
    for copy in pending[len(pending) - (nr - 1):]:
        copy.wait_recv()
    for d in range(1, nr):
        image = image + img_in[d - 1]
    out_ref[...] = image
    for copy in pending:
        copy.wait_send()
    pltpu.make_async_copy(told, told, es).wait()


def local(src_green, rcv_green, model, observed):
    n = lax.axis_size("pts")
    nr = lax.axis_size("rcv")
    bits = n.bit_length() - 1
    nx = 2 ** ((bits + 1) // 4)
    if n % nx:
        nx = 1
    nz = n // nx
    sources, points = src_green.shape[1:]
    receivers = rcv_green.shape[1]
    block = observed.shape[0]
    scale = math.sqrt(points * n / (receivers * nr * sources))
    f32, bf16 = jnp.float32, jnp.bfloat16
    dma = pltpu.SemaphoreType.DMA
    halves = 2 if receivers % 256 == 0 else 1
    width = receivers // halves
    lanes = 128 if width % 128 == 0 else width
    image = pl.pallas_call(
        functools.partial(kernel, nx, nz, nr, scale),
        out_shape=jax.ShapeDtypeStruct((1, points), f32),
        in_specs=[pl.BlockSpec(memory_space=pl.ANY)] * 4,
        out_specs=pl.BlockSpec(memory_space=pltpu.VMEM),
        scratch_shapes=[
            pltpu.VMEM(src_green.shape, f32),
            pltpu.VMEM(rcv_green.shape, f32),
            pltpu.VMEM((1, points), f32),
            pltpu.VMEM(observed.shape, f32),
            pltpu.VMEM(rcv_green.shape, bf16),
            pltpu.VMEM(rcv_green.shape, bf16),
            pltpu.VMEM((nx, nz, halves, 2, block, width), f32),
            pltpu.VMEM((max(nx - 1, 1), nz, halves, 2, block, width), f32),
            pltpu.VMEM((nz, halves, 2, block, width), f32),
            pltpu.VMEM((nz, halves, 2, block, width), f32),
            pltpu.VMEM((nx, nz, halves, 2, block, width), f32),
            pltpu.VMEM((1, 1, lanes), f32),
            pltpu.VMEM((n * nr, 1, lanes), f32),
            pltpu.VMEM((1, 1, points), f32),
            pltpu.VMEM((max(nr - 1, 1), 1, points), f32),
            dma((3 + halves,)),
            dma((max(nx - 1, 1), nz, halves)),
            dma((max(nx - 1, 1), nz, halves)),
            dma((nz, halves)),
            dma((nz, halves)),
            dma((nz, halves)),
            dma((nz, halves)),
            dma((max(nx - 1, 1), nz, halves)),
            dma((max(nx - 1, 1), nz, halves)),
            dma(()),
            dma(()),
            dma((max(nr - 1, 1),)),
            dma((max(nr - 1, 1),)),
            pltpu.SemaphoreType.REGULAR((2,)),
        ],
        compiler_params=pltpu.CompilerParams(collective_id=0, has_side_effects=True),
    )(src_green, rcv_green, model.reshape(1, points), observed)
    return image.reshape(points)


def solution(mesh):
    placed = (
        P(None, "grp", "pts"),
        P(None, ("grp", "rcv"), "pts"),
        P(("grp", "pts")),
        P(("grp", "pts"), None, "rcv"),
    )
    return jax.shard_map(
        local, mesh=mesh, in_specs=placed, out_specs=P(("grp", "pts")), check_vma=False
    )
```

```python
import functools
import math

import jax
import jax.numpy as jnp
from jax import lax
from jax.experimental import pallas as pl
from jax.experimental.pallas import tpu as pltpu
from jax.sharding import PartitionSpec as P

MESH = pl.DeviceIdType.MESH
UNROLL = 32


def repeat(start, stop, body):
    if stop - start <= UNROLL:
        for i in range(start, stop):
            body(i)
    else:

        @pl.loop(start, stop)
        def _(i):
            body(i)


def split(a):
    high = a.astype(jnp.bfloat16)
    low = (a - high.astype(jnp.float32)).astype(jnp.bfloat16)
    return high, low


def product(a, b_high, b_low, b_axis):
    rows = a.shape[0]
    a_high, a_low = split(a)
    dims = (((1,), (b_axis,)), ((), ()))
    both = lax.dot_general(
        jnp.concatenate([a_high, a_low], axis=0), b_high, dims, preferred_element_type=jnp.float32
    )
    cross = lax.dot_general(a_high, b_low, dims, preferred_element_type=jnp.float32)
    return both[:rows] + (both[rows:] + cross)


def near_first(z, nz):
    if nz > 8:
        return [jnp.int32(j) for j in range(1, nz)]
    table = []
    for here in range(nz):
        others = sorted((abs(o - here), o) for o in range(nz) if o != here)
        table.append([(o - here) % nz for _, o in others])
    order = []
    for k in range(nz - 1):
        j = jnp.int32(table[0][k])
        for here in range(1, nz):
            j = jnp.where(z == here, jnp.int32(table[here][k]), j)
        order.append(j)
    return order


def kernel(
    nx, nz, nr, scale,
    src_hbm, rcv_hbm, model_hbm, obs_hbm, out_ref,
    src, rcv, model, obs, b_high, b_low, part, xbuf, zsend, zbuf, gath, own_energy, ebuf, img, img_in,
    load, xs, xr, zs, zr, gs, gr, hs, hr, es, er, ims, imr, tokens,
):
    n = nx * nz
    total = n * nr
    p = lax.axis_index("pts")
    c = lax.axis_index("rcv")
    z, x = p // nx, p % nx
    q = p * nr + c
    sources = src.shape[1]
    receivers = rcv.shape[1]
    block = part.shape[3]

    loads = [
        pltpu.make_async_copy(src_hbm, src, load.at[0]),
        pltpu.make_async_copy(model_hbm, model, load.at[1]),
        pltpu.make_async_copy(rcv_hbm.at[0], rcv.at[0], load.at[2]),
        pltpu.make_async_copy(rcv_hbm.at[1], rcv.at[1], load.at[3]),
        pltpu.make_async_copy(obs_hbm, obs, load.at[4]),
    ]
    for copy in loads:
        copy.start()

    barrier = pltpu.get_barrier_semaphore()
    row_peers = nx * nr - 1
    below, above = (z + nz - 1) % nz, (z + 1) % nz

    def greet(device):
        pl.semaphore_signal(barrier, inc=1, device_id=device, device_id_type=MESH)

    for o in range(1, nx * nr):
        to = (x * nr + c + o) % (nx * nr)
        greet({"pts": z * nx + to // nr, "rcv": to % nr})

    @pl.when(z > 0)
    def _():
        greet({"pts": below * nx + x})

    @pl.when(z < nz - 1)
    def _():
        greet({"pts": above * nx + x})

    def pass_up():
        @pl.when(z > 0)
        def _():
            pl.semaphore_wait(tokens.at[0], 1)

        @pl.when(z < nz - 1)
        def _():
            pl.semaphore_signal(tokens.at[0], inc=1, device_id={"pts": above * nx + x}, device_id_type=MESH)

    def pass_down():
        @pl.when(z < nz - 1)
        def _():
            pl.semaphore_wait(tokens.at[1], 1)

        @pl.when(z > 0)
        def _():
            pl.semaphore_signal(tokens.at[1], inc=1, device_id={"pts": below * nx + x}, device_id_type=MESH)

    for copy in loads[:3]:
        copy.wait()
    b_high[0], b_low[0] = split(rcv[0])
    loads[3].wait()
    b_high[1], b_low[1] = split(rcv[1])

    rows = nz * block

    def sources_of(part_of, d):
        column = (x + d) % nx
        return jnp.concatenate(
            [src[part_of, pl.ds(pl.multiple_of((k * nx + column) * block, block), block)] for k in range(nz)],
            axis=0,
        )

    def model_column(d):
        weight = model[...]
        scaled = jnp.concatenate([sources_of(0, d) * weight, sources_of(1, d) * weight], axis=0)
        with_real = product(scaled, b_high[0], b_low[0], 1)
        with_imag = product(scaled, b_high[1], b_low[1], 1)
        part[d, :, 0] = (with_real[:rows] - with_imag[rows:]).reshape(nz, block, receivers)
        part[d, :, 1] = (with_imag[:rows] + with_real[rows:]).reshape(nz, block, receivers)

    order = near_first(z, nz)
    far = order[::-1]

    def to_x(source, target, send, recv, d):
        return pltpu.make_async_remote_copy(
            source, target, send, recv,
            device_id={"pts": z * nx + (x + d) % nx}, device_id_type=MESH,
        )

    def to_z(source, target, send, recv, j):
        return pltpu.make_async_remote_copy(
            source, target, send, recv,
            device_id={"pts": ((z + j) % nz) * nx + x}, device_id_type=MESH,
        )

    pending = []
    x_copies = [[] for _ in range(nz)]
    for d in range(1, nx):
        model_column(d)
        if d == 1:
            pl.semaphore_wait(barrier, row_peers + jnp.minimum(z, 1) + jnp.minimum(nz - 1 - z, 1))
        for k, j in enumerate(far + [jnp.int32(0)]):
            copy = to_x(part.at[d, (z + j) % nz], xbuf.at[d - 1, j], xs.at[d - 1, j], xr.at[d - 1, j], d)
            copy.start()
            x_copies[k].append(copy)
    model_column(0)
    if nx == 1:
        pl.semaphore_wait(barrier, row_peers + jnp.minimum(z, 1) + jnp.minimum(nz - 1 - z, 1))

    @pl.when(z < nz // 2)
    def _():
        pass_up()
        pass_down()

    @pl.when(z >= nz // 2)
    def _():
        pass_down()
        pass_up()

    loads[4].wait()
    observed = [obs[:, part_of, :] for part_of in range(2)]
    z_copies = []
    for j, row in zip(far, x_copies):
        acc = part[0, (z + j) % nz]
        for d, copy in enumerate(row):
            copy.wait_recv()
            acc = acc + xbuf[d, j]
        zsend[j] = acc
        copy = to_z(zsend.at[j], zbuf.at[j], zs.at[j], zr.at[j], j)
        copy.start()
        z_copies.append(copy)
    acc = part[0, z]
    for d, copy in enumerate(x_copies[-1]):
        copy.wait_recv()
        acc = acc + xbuf[d, 0]
    back = [(nz - j) % nz for j in order]
    for j in back:
        to_z(zsend.at[j], zbuf.at[j], zs.at[j], zr.at[j], j).wait_recv()
        acc = acc + zbuf[j]
    for row in x_copies:
        pending += row
    pending += z_copies

    real = acc[0] - observed[0]
    imag = acc[1] - observed[1]
    gath[0, z, 0] = real
    gath[0, z, 1] = imag
    lanes = own_energy.shape[-1]
    energy = jnp.sum(real * real + imag * imag, axis=0, keepdims=True)
    narrow = energy[:, :lanes]
    for i in range(1, receivers // lanes):
        narrow = narrow + energy[:, i * lanes:(i + 1) * lanes]
    own_energy[0] = narrow

    at_end = jnp.logical_or(z == 0, z == nz - 1) if 1 < nz <= 8 else z < 0
    across = []
    for d in range(1, nx):
        goal = ((z + far[0]) % nz) * nx + (x + d) % nx
        across.append(pltpu.make_async_remote_copy(
            gath.at[0, z], gath.at[d, z], hs.at[d - 1, back[-1]], hr.at[d - 1, far[0]],
            device_id={"pts": goal}, device_id_type=MESH,
        ))

    @pl.when(at_end)
    def _():
        for copy in across:
            copy.start()

    for j in far:
        copy = to_z(gath.at[0, z], gath.at[0, z], gs.at[j], gr.at[j], j)
        copy.start()
        pending.append(copy)
    for d in range(1, nx):
        copy = to_x(gath.at[0, z], gath.at[d, z], hs.at[d - 1, 0], hr.at[d - 1, 0], d)
        copy.start()
        pending.append(copy)

    def tell(o):
        to = (q + o) % total
        pltpu.make_async_remote_copy(
            own_energy.at[0], ebuf.at[o - 1], es, er,
            device_id={"pts": to // nr, "rcv": to % nr}, device_id_type=MESH,
        ).start()

    repeat(1, total, tell)

    for j in back:
        origin = (z - j + nz) % nz
        to_z(gath.at[0, origin], gath.at[0, origin], gs.at[j], gr.at[j], j).wait_recv()
        for d in range(1, nx):
            copy = to_x(gath.at[0, origin], gath.at[d, origin], hs.at[d - 1, j], hr.at[d - 1, j], d)
            if j is back[-1]:
                pl.when(jnp.logical_not(at_end))(copy.start)
            else:
                copy.start()
            pending.append(copy)
    told = ebuf.at[pl.ds(0, total - 1)]
    pltpu.make_async_copy(told, told, er).wait()
    summed = jnp.sum(jnp.sum(ebuf[pl.ds(0, total - 1)], axis=0) + own_energy[0], axis=1, keepdims=True)
    spread_sq = summed / (sources * receivers * nr) + 1e-06
    inverse = 1.0 / spread_sq

    def image_column(d):
        real = gath[d, :, 0].reshape(rows, receivers)
        imag = gath[d, :, 1].reshape(rows, receivers)
        gain = 1.0 / (1.0 + (real * real + imag * imag) * inverse)
        weighted = jnp.concatenate([real * gain, imag * gain], axis=0)
        with_real = product(weighted, b_high[0], b_low[0], 0)
        with_imag = product(weighted, b_high[1], b_low[1], 0)
        back_real = with_real[:rows] + with_imag[rows:]
        back_imag = with_real[rows:] - with_imag[:rows]
        terms = sources_of(0, nx - d) * back_real + sources_of(1, nx - d) * back_imag
        return jnp.sum(terms, axis=0, keepdims=True)

    image = image_column(0)
    for d in range(1, nx):
        for j in [jnp.int32(0)] + back:
            origin = (z - j + nz) % nz
            to_x(gath.at[0, origin], gath.at[d, origin], hs.at[d - 1, j], hr.at[d - 1, j], d).wait_recv()
        image = image + image_column(d)
    image = image * scale
    img[0] = image
    for d in range(1, nr):
        copy = pltpu.make_async_remote_copy(
            img.at[0], img_in.at[d - 1], ims.at[d - 1], imr.at[d - 1],
            device_id={"rcv": (c + d) % nr}, device_id_type=MESH,
        )
        copy.start()
        pending.append(copy)
    for copy in pending[len(pending) - (nr - 1):]:
        copy.wait_recv()
    for d in range(1, nr):
        image = image + img_in[d - 1]
    out_ref[...] = image
    for copy in pending:
        copy.wait_send()
    pltpu.make_async_copy(told, told, es).wait()


def local(src_green, rcv_green, model, observed):
    n = lax.axis_size("pts")
    nr = lax.axis_size("rcv")
    bits = n.bit_length() - 1
    nx = 2 ** ((bits + 1) // 4)
    if n % nx:
        nx = 1
    nz = n // nx
    sources, points = src_green.shape[1:]
    receivers = rcv_green.shape[1]
    block = observed.shape[0]
    scale = math.sqrt(points * n / (receivers * nr * sources))
    f32, bf16 = jnp.float32, jnp.bfloat16
    dma = pltpu.SemaphoreType.DMA
    lanes = 128 if receivers % 128 == 0 else receivers
    image = pl.pallas_call(
        functools.partial(kernel, nx, nz, nr, scale),
        out_shape=jax.ShapeDtypeStruct((1, points), f32),
        in_specs=[pl.BlockSpec(memory_space=pl.ANY)] * 4,
        out_specs=pl.BlockSpec(memory_space=pltpu.VMEM),
        scratch_shapes=[
            pltpu.VMEM(src_green.shape, f32),
            pltpu.VMEM(rcv_green.shape, f32),
            pltpu.VMEM((1, points), f32),
            pltpu.VMEM(observed.shape, f32),
            pltpu.VMEM(rcv_green.shape, bf16),
            pltpu.VMEM(rcv_green.shape, bf16),
            pltpu.VMEM((nx, nz, 2, block, receivers), f32),
            pltpu.VMEM((max(nx - 1, 1), nz, 2, block, receivers), f32),
            pltpu.VMEM((nz, 2, block, receivers), f32),
            pltpu.VMEM((nz, 2, block, receivers), f32),
            pltpu.VMEM((nx, nz, 2, block, receivers), f32),
            pltpu.VMEM((1, 1, lanes), f32),
            pltpu.VMEM((n * nr, 1, lanes), f32),
            pltpu.VMEM((1, 1, points), f32),
            pltpu.VMEM((max(nr - 1, 1), 1, points), f32),
            dma((5,)),
            dma((max(nx - 1, 1), nz)),
            dma((max(nx - 1, 1), nz)),
            dma((nz,)),
            dma((nz,)),
            dma((nz,)),
            dma((nz,)),
            dma((max(nx - 1, 1), nz)),
            dma((max(nx - 1, 1), nz)),
            dma(()),
            dma(()),
            dma((max(nr - 1, 1),)),
            dma((max(nr - 1, 1),)),
            pltpu.SemaphoreType.REGULAR((2,)),
        ],
        compiler_params=pltpu.CompilerParams(collective_id=0, has_side_effects=True),
    )(src_green, rcv_green, model.reshape(1, points), observed)
    return image.reshape(points)


def solution(mesh):
    placed = (
        P(None, "grp", "pts"),
        P(None, ("grp", "rcv"), "pts"),
        P(("grp", "pts")),
        P(("grp", "pts"), None, "rcv"),
    )
    return jax.shard_map(
        local, mesh=mesh, in_specs=placed, out_specs=P(("grp", "pts")), check_vma=False
    )
```

```python
import functools
import math

import jax
import jax.numpy as jnp
from jax import lax
from jax.experimental import pallas as pl
from jax.experimental.pallas import tpu as pltpu
from jax.sharding import PartitionSpec as P

MESH = pl.DeviceIdType.MESH
UNROLL = 32


def repeat(start, stop, body):
    if stop - start <= UNROLL:
        for i in range(start, stop):
            body(i)
    else:

        @pl.loop(start, stop)
        def _(i):
            body(i)


def split(a):
    high = a.astype(jnp.bfloat16)
    low = (a - high.astype(jnp.float32)).astype(jnp.bfloat16)
    return high, low


def product(a, b_high, b_low, b_axis):
    rows = a.shape[0]
    a_high, a_low = split(a)
    dims = (((1,), (b_axis,)), ((), ()))
    both = lax.dot_general(
        jnp.concatenate([a_high, a_low], axis=0), b_high, dims, preferred_element_type=jnp.float32
    )
    cross = lax.dot_general(a_high, b_low, dims, preferred_element_type=jnp.float32)
    return both[:rows] + (both[rows:] + cross)


def near_first(z, nz):
    if nz > 8:
        return [jnp.int32(j) for j in range(1, nz)]
    table = []
    for here in range(nz):
        others = sorted((abs(o - here), o) for o in range(nz) if o != here)
        table.append([(o - here) % nz for _, o in others])
    order = []
    for k in range(nz - 1):
        j = jnp.int32(table[0][k])
        for here in range(1, nz):
            j = jnp.where(z == here, jnp.int32(table[here][k]), j)
        order.append(j)
    return order


def kernel(
    nx, nz, nr, scale,
    src_hbm, rcv_hbm, model_hbm, obs_hbm, out_ref,
    src, rcv, model, obs, b_high, b_low, part, xbuf, zsend, zbuf, gath, own_energy, ebuf, img, img_in,
    load, xs, xr, zs, zr, gs, gr, hs, hr, es, er, ims, imr, tokens, dbuf, dr,
):
    n = nx * nz
    total = n * nr
    p = lax.axis_index("pts")
    c = lax.axis_index("rcv")
    z, x = p // nx, p % nx
    q = p * nr + c
    sources = src.shape[1]
    receivers = rcv.shape[1]
    block = part.shape[3]

    loads = [
        pltpu.make_async_copy(src_hbm, src, load.at[0]),
        pltpu.make_async_copy(model_hbm, model, load.at[1]),
        pltpu.make_async_copy(rcv_hbm.at[0], rcv.at[0], load.at[2]),
        pltpu.make_async_copy(rcv_hbm.at[1], rcv.at[1], load.at[3]),
        pltpu.make_async_copy(obs_hbm, obs, load.at[4]),
    ]
    for copy in loads:
        copy.start()

    barrier = pltpu.get_barrier_semaphore()
    row_peers = nx * nr - 1
    below, above = (z + nz - 1) % nz, (z + 1) % nz

    def greet(device):
        pl.semaphore_signal(barrier, inc=1, device_id=device, device_id_type=MESH)

    for o in range(1, nx * nr):
        to = (x * nr + c + o) % (nx * nr)
        greet({"pts": z * nx + to // nr, "rcv": to % nr})

    @pl.when(z > 0)
    def _():
        greet({"pts": below * nx + x})

    @pl.when(z < nz - 1)
    def _():
        greet({"pts": above * nx + x})

    def pass_up():
        @pl.when(z > 0)
        def _():
            pl.semaphore_wait(tokens.at[0], 1)

        @pl.when(z < nz - 1)
        def _():
            pl.semaphore_signal(tokens.at[0], inc=1, device_id={"pts": above * nx + x}, device_id_type=MESH)

    def pass_down():
        @pl.when(z < nz - 1)
        def _():
            pl.semaphore_wait(tokens.at[1], 1)

        @pl.when(z > 0)
        def _():
            pl.semaphore_signal(tokens.at[1], inc=1, device_id={"pts": below * nx + x}, device_id_type=MESH)

    for copy in loads[:3]:
        copy.wait()
    b_high[0], b_low[0] = split(rcv[0])
    loads[3].wait()
    b_high[1], b_low[1] = split(rcv[1])

    rows = nz * block

    def sources_of(part_of, d):
        column = (x + d) % nx
        return jnp.concatenate(
            [src[part_of, pl.ds(pl.multiple_of((k * nx + column) * block, block), block)] for k in range(nz)],
            axis=0,
        )

    def model_column(d):
        weight = model[...]
        scaled = jnp.concatenate([sources_of(0, d) * weight, sources_of(1, d) * weight], axis=0)
        with_real = product(scaled, b_high[0], b_low[0], 1)
        with_imag = product(scaled, b_high[1], b_low[1], 1)
        part[d, :, 0] = (with_real[:rows] - with_imag[rows:]).reshape(nz, block, receivers)
        part[d, :, 1] = (with_imag[:rows] + with_real[rows:]).reshape(nz, block, receivers)

    order = near_first(z, nz)
    far = order[::-1]

    def to_x(source, target, send, recv, d):
        return pltpu.make_async_remote_copy(
            source, target, send, recv,
            device_id={"pts": z * nx + (x + d) % nx}, device_id_type=MESH,
        )

    def to_z(source, target, send, recv, j):
        return pltpu.make_async_remote_copy(
            source, target, send, recv,
            device_id={"pts": ((z + j) % nz) * nx + x}, device_id_type=MESH,
        )

    at_end = jnp.logical_or(z == 0, z == nz - 1) if 1 < nz <= 8 else z < 0
    pending = []
    x_copies = [[] for _ in range(nz)]
    for d in range(1, nx):
        model_column(d)
        if d == 1:
            pl.semaphore_wait(barrier, row_peers + jnp.minimum(z, 1) + jnp.minimum(nz - 1 - z, 1))
        for k, j in enumerate(far + [jnp.int32(0)]):
            copy = to_x(part.at[d, (z + j) % nz], xbuf.at[d - 1, j], xs.at[d - 1, j], xr.at[d - 1, j], d)
            if k == 0 and nz > 1:
                pl.when(jnp.logical_not(at_end))(copy.start)
            else:
                copy.start()
            x_copies[k].append(copy)
    model_column(0)
    if nx == 1:
        pl.semaphore_wait(barrier, row_peers + jnp.minimum(z, 1) + jnp.minimum(nz - 1 - z, 1))

    @pl.when(z < nz // 2)
    def _():
        pass_up()
        pass_down()

    @pl.when(z >= nz // 2)
    def _():
        pass_down()
        pass_up()

    loads[4].wait()
    observed = [obs[:, part_of, :] for part_of in range(2)]
    z_copies = []
    if nz > 1:

        @pl.when(at_end)
        def _():
            for d in range(1, nx):
                goal = ((z + far[0]) % nz) * nx + (x + d) % nx
                pltpu.make_async_remote_copy(
                    part.at[d, (z + far[0]) % nz], dbuf.at[d - 1], xs.at[d - 1, far[0]], dr.at[d - 1],
                    device_id={"pts": goal}, device_id_type=MESH,
                ).start()

    for k, (j, row) in enumerate(zip(far, x_copies)):
        if k == 0:
            zsend[j] = part[0, (z + j) % nz]

            @pl.when(jnp.logical_not(at_end))
            def _(j=j, row=row):
                for d, copy in enumerate(row):
                    copy.wait_recv()
                    zsend[j] = zsend[j] + xbuf[d, j]

            copy = to_z(zsend.at[j], zbuf.at[j], zs.at[j], zr.at[j], j)
            copy.start()
            z_copies.append(copy)
            continue
        acc = part[0, (z + j) % nz]
        for d, copy in enumerate(row):
            copy.wait_recv()
            acc = acc + xbuf[d, j]
        zsend[j] = acc
        copy = to_z(zsend.at[j], zbuf.at[j], zs.at[j], zr.at[j], j)
        copy.start()
        z_copies.append(copy)
    acc = part[0, z]
    for d, copy in enumerate(x_copies[-1]):
        copy.wait_recv()
        acc = acc + xbuf[d, 0]
    back = [(nz - j) % nz for j in order]
    for j in back:
        to_z(zsend.at[j], zbuf.at[j], zs.at[j], zr.at[j], j).wait_recv()
        acc = acc + zbuf[j]
    if nz > 1:
        zsend[0] = acc

        @pl.when(at_end)
        def _():
            for d in range(1, nx):
                pltpu.make_async_copy(dbuf.at[d - 1], dbuf.at[d - 1], dr.at[d - 1]).wait()
                zsend[0] = zsend[0] + dbuf[d - 1]

        acc = zsend[0]
    for row in x_copies:
        pending += row
    pending += z_copies

    real = acc[0] - observed[0]
    imag = acc[1] - observed[1]
    gath[0, z, 0] = real
    gath[0, z, 1] = imag
    lanes = own_energy.shape[-1]
    energy = jnp.sum(real * real + imag * imag, axis=0, keepdims=True)
    narrow = energy[:, :lanes]
    for i in range(1, receivers // lanes):
        narrow = narrow + energy[:, i * lanes:(i + 1) * lanes]
    own_energy[0] = narrow

    across = []
    for d in range(1, nx):
        goal = ((z + far[0]) % nz) * nx + (x + d) % nx
        across.append(pltpu.make_async_remote_copy(
            gath.at[0, z], gath.at[d, z], hs.at[d - 1, back[-1]], hr.at[d - 1, far[0]],
            device_id={"pts": goal}, device_id_type=MESH,
        ))

    @pl.when(at_end)
    def _():
        for copy in across:
            copy.start()

    for j in far:
        copy = to_z(gath.at[0, z], gath.at[0, z], gs.at[j], gr.at[j], j)
        copy.start()
        pending.append(copy)
    for d in range(1, nx):
        copy = to_x(gath.at[0, z], gath.at[d, z], hs.at[d - 1, 0], hr.at[d - 1, 0], d)
        copy.start()
        pending.append(copy)

    def tell(o):
        to = (q + o) % total
        pltpu.make_async_remote_copy(
            own_energy.at[0], ebuf.at[o - 1], es, er,
            device_id={"pts": to // nr, "rcv": to % nr}, device_id_type=MESH,
        ).start()

    repeat(1, total, tell)

    for j in back:
        origin = (z - j + nz) % nz
        to_z(gath.at[0, origin], gath.at[0, origin], gs.at[j], gr.at[j], j).wait_recv()
        for d in range(1, nx):
            copy = to_x(gath.at[0, origin], gath.at[d, origin], hs.at[d - 1, j], hr.at[d - 1, j], d)
            if j is back[-1]:
                pl.when(jnp.logical_not(at_end))(copy.start)
            else:
                copy.start()
            pending.append(copy)
    told = ebuf.at[pl.ds(0, total - 1)]
    pltpu.make_async_copy(told, told, er).wait()
    summed = jnp.sum(jnp.sum(ebuf[pl.ds(0, total - 1)], axis=0) + own_energy[0], axis=1, keepdims=True)
    spread_sq = summed / (sources * receivers * nr) + 1e-06
    inverse = 1.0 / spread_sq

    def image_column(d):
        real = gath[d, :, 0].reshape(rows, receivers)
        imag = gath[d, :, 1].reshape(rows, receivers)
        gain = 1.0 / (1.0 + (real * real + imag * imag) * inverse)
        weighted = jnp.concatenate([real * gain, imag * gain], axis=0)
        with_real = product(weighted, b_high[0], b_low[0], 0)
        with_imag = product(weighted, b_high[1], b_low[1], 0)
        back_real = with_real[:rows] + with_imag[rows:]
        back_imag = with_real[rows:] - with_imag[:rows]
        terms = sources_of(0, nx - d) * back_real + sources_of(1, nx - d) * back_imag
        return jnp.sum(terms, axis=0, keepdims=True)

    image = image_column(0)
    for d in range(1, nx):
        for j in [jnp.int32(0)] + back:
            origin = (z - j + nz) % nz
            to_x(gath.at[0, origin], gath.at[d, origin], hs.at[d - 1, j], hr.at[d - 1, j], d).wait_recv()
        image = image + image_column(d)
    image = image * scale
    img[0] = image
    for d in range(1, nr):
        copy = pltpu.make_async_remote_copy(
            img.at[0], img_in.at[d - 1], ims.at[d - 1], imr.at[d - 1],
            device_id={"rcv": (c + d) % nr}, device_id_type=MESH,
        )
        copy.start()
        pending.append(copy)
    for copy in pending[len(pending) - (nr - 1):]:
        copy.wait_recv()
    for d in range(1, nr):
        image = image + img_in[d - 1]
    out_ref[...] = image
    for copy in pending:
        copy.wait_send()
    pltpu.make_async_copy(told, told, es).wait()


def local(src_green, rcv_green, model, observed):
    n = lax.axis_size("pts")
    nr = lax.axis_size("rcv")
    bits = n.bit_length() - 1
    nx = 2 ** ((bits + 1) // 4)
    if n % nx:
        nx = 1
    nz = n // nx
    sources, points = src_green.shape[1:]
    receivers = rcv_green.shape[1]
    block = observed.shape[0]
    scale = math.sqrt(points * n / (receivers * nr * sources))
    f32, bf16 = jnp.float32, jnp.bfloat16
    dma = pltpu.SemaphoreType.DMA
    lanes = 128 if receivers % 128 == 0 else receivers
    image = pl.pallas_call(
        functools.partial(kernel, nx, nz, nr, scale),
        out_shape=jax.ShapeDtypeStruct((1, points), f32),
        in_specs=[pl.BlockSpec(memory_space=pl.ANY)] * 4,
        out_specs=pl.BlockSpec(memory_space=pltpu.VMEM),
        scratch_shapes=[
            pltpu.VMEM(src_green.shape, f32),
            pltpu.VMEM(rcv_green.shape, f32),
            pltpu.VMEM((1, points), f32),
            pltpu.VMEM(observed.shape, f32),
            pltpu.VMEM(rcv_green.shape, bf16),
            pltpu.VMEM(rcv_green.shape, bf16),
            pltpu.VMEM((nx, nz, 2, block, receivers), f32),
            pltpu.VMEM((max(nx - 1, 1), nz, 2, block, receivers), f32),
            pltpu.VMEM((nz, 2, block, receivers), f32),
            pltpu.VMEM((nz, 2, block, receivers), f32),
            pltpu.VMEM((nx, nz, 2, block, receivers), f32),
            pltpu.VMEM((1, 1, lanes), f32),
            pltpu.VMEM((n * nr, 1, lanes), f32),
            pltpu.VMEM((1, 1, points), f32),
            pltpu.VMEM((max(nr - 1, 1), 1, points), f32),
            dma((5,)),
            dma((max(nx - 1, 1), nz)),
            dma((max(nx - 1, 1), nz)),
            dma((nz,)),
            dma((nz,)),
            dma((nz,)),
            dma((nz,)),
            dma((max(nx - 1, 1), nz)),
            dma((max(nx - 1, 1), nz)),
            dma(()),
            dma(()),
            dma((max(nr - 1, 1),)),
            dma((max(nr - 1, 1),)),
            pltpu.SemaphoreType.REGULAR((2,)),
            pltpu.VMEM((max(nx - 1, 1), 2, block, receivers), f32),
            dma((max(nx - 1, 1),)),
        ],
        compiler_params=pltpu.CompilerParams(collective_id=0, has_side_effects=True),
    )(src_green, rcv_green, model.reshape(1, points), observed)
    return image.reshape(points)


def solution(mesh):
    placed = (
        P(None, "grp", "pts"),
        P(None, ("grp", "rcv"), "pts"),
        P(("grp", "pts")),
        P(("grp", "pts"), None, "rcv"),
    )
    return jax.shard_map(
        local, mesh=mesh, in_specs=placed, out_specs=P(("grp", "pts")), check_vma=False
    )
```
